32 devices in a mesh: row: 4 (over x, core), col: 8 (over z, y).
Axes of the slice: x: 2, y: 2, z: 4, core: 2. Of those that a mesh axis runs over, the one named last changes fastest.
Arguments:
- signatures: bfloat16 [2048, 49152], P('row', 'col'), as said below
- trailing: float32 [2048, 1024], P('row', 'col'), may hold values from -6 to 6
- ridge: float32 [1], replicated, may hold values from 0.5 to 2
- panel_index: int32 [1], replicated, may hold values from 1 to 3
Outputs:
- factor: float32 [2048, 256], P(('row', 'col'))
- updated: float32 [2048, 1024], P('row', 'col')
The draws below stay inside these ranges and needn't reach their ends.
Inputs may be any that keep to these rules, and one draw needn't show every extreme that they name: `signatures`: every diagonal block of the Gram matrix plus the ridge is positive definite.
All inputs are finite; a program needn't handle non-finite values.
Results may differ from the reference program's by a relative error of at most 0.0003.
Values may be sent and summed in bfloat16 or wider, within the bound.
A program may use at most 64 MiB of HBM per device.

```python
import math
import jax
import jax.numpy as jnp
from jax import lax

PANEL = 256
FEATURES = 49152
ROWS_DEV = 512
ORDER = 2048
WINDOW = 1024


def draw_signatures(key, part):
    keys = jax.random.split(jax.random.fold_in(key, 7), 6)
    noise = jax.random.normal(keys[0], (ORDER, FEATURES), jnp.float32)
    scales = jnp.exp(jax.random.uniform(keys[1], (ORDER, 1), jnp.float32, -0.7, 0.7))
    mixing = jax.random.normal(keys[2], (ORDER, PANEL), jnp.float32)
    shared = jax.random.normal(keys[3], (ORDER, 1), jnp.float32) * jax.random.normal(keys[4], (1, PANEL), jnp.float32)
    mixing = mixing + 0.7 * shared
    pattern = jax.random.normal(keys[5], (PANEL, FEATURES // PANEL), jnp.float32)
    common = (mixing[:, :, None] * pattern[None, :, :]).reshape(ORDER, FEATURES)
    values = (scales * noise + common) / jnp.sqrt(jnp.float32(FEATURES))
    return values.astype(jnp.bfloat16)


def block_levels(rng, dims, pieces, smallest, high):
    loudness, own = 1.0, jax.random.fold_in(rng, 6)
    for position, parts in pieces:
        steps = jnp.exp(jax.random.uniform(jax.random.fold_in(own, position), (parts,), jnp.float32, smallest / len(pieces), high / len(pieces)))
        loudness = loudness * jnp.repeat(steps, dims[position] // parts).reshape([-1 if axis == position else 1 for axis in range(len(dims))])
    return loudness


def normal_values(key, shape, spread, bound, pieces=(), kind=jnp.bfloat16):
    gain = block_levels(key, shape, pieces, -0.22, 0.18) if pieces else 1.0
    drawn = jax.random.normal(key, shape, jnp.float32) * spread * gain
    return jnp.minimum(jnp.maximum(drawn, -bound), bound).astype(kind)


def setup_inputs(seed: int = 0) -> dict:
    key_list = jax.random.split(jax.random.key(seed), 5)
    signatures = draw_signatures(jax.random.fold_in(key_list[4], 71), 0)
    trailing = normal_values(key_list[1], (ORDER, WINDOW), 1.0, 6.0, ((0, 4), (1, 8)), jnp.float32)
    ridge = jnp.clip(jnp.exp(jax.random.uniform(key_list[2], (1,), jnp.float32, math.log(0.5), math.log(2.0))), 0.5, 2.0)
    panel_index = jax.random.randint(key_list[3], (1,), 1, (ORDER - WINDOW) // PANEL).astype(jnp.int32)
    return dict(signatures=signatures, trailing=trailing, ridge=ridge, panel_index=panel_index)


def add_ridge(block, first_row, panel_start, ridge):
    row_ids = first_row + lax.broadcasted_iota(jnp.int32, block.shape, 0)
    col_ids = panel_start + lax.broadcasted_iota(jnp.int32, block.shape, 1)
    return block + jnp.where(row_ids == col_ids, ridge[0], jnp.zeros((), block.dtype))

def reference(signatures, trailing, ridge, panel_index):
    panel_start = (panel_index[0] * PANEL).astype(jnp.int32)
    panel_paths = lax.dynamic_slice_in_dim(signatures, panel_start, PANEL, 0)
    row_blocks = signatures.reshape(ORDER // ROWS_DEV, ROWS_DEV, FEATURES)

    def block_product(row_block):
        return lax.dot_general(row_block.astype(jnp.float32), panel_paths.astype(jnp.float32), (((1,), (1,)), ((), ())), preferred_element_type=jnp.float32)
    panel_cols = lax.map(block_product, row_blocks).reshape(ORDER, PANEL)
    panel_cols = add_ridge(panel_cols, jnp.int32(0), panel_start, ridge)
    diagonal = lax.dynamic_slice_in_dim(panel_cols, panel_start, PANEL, 0)
    lower = jnp.linalg.cholesky(diagonal)
    factor = jax.scipy.linalg.solve_triangular(lower, panel_cols.T, lower=True).T
    row_ids = lax.broadcasted_iota(jnp.int32, factor.shape, 0)
    factor = jnp.where(row_ids >= panel_start, factor, jnp.zeros((), factor.dtype))
    trailing_start = (panel_start + PANEL).astype(jnp.int32)
    window_rows = lax.dynamic_slice_in_dim(factor, trailing_start, WINDOW, 0)
    updated = trailing - lax.dot_general(factor.astype(jnp.float32), window_rows.astype(jnp.float32), (((1,), (1,)), ((), ())), precision=lax.Precision.HIGHEST, preferred_element_type=jnp.float32)
    return (factor, updated)
```

```python
import functools

import jax
import jax.numpy as jnp
from jax import lax
from jax.experimental import pallas as pl
from jax.experimental.pallas import tpu as pltpu
from jax.sharding import PartitionSpec as P

PANEL = 256
CORES = 2
MESH = pl.DeviceIdType.MESH
NT = (((1,), (1,)), ((), ()))
NN = (((1,), (0,)), ((), ()))


def remote(src, dst, send, recv, axis, where):
    return pltpu.make_async_remote_copy(
        src_ref=src, dst_ref=dst, send_sem=send, recv_sem=recv, device_id={axis: where}, device_id_type=MESH
    )


def gram_kernel(
    index, rows_count, col_count, steps, tile,
    sig_ref, gram_ref, window_ref, diagonal_ref,
    sig, panel, part, shares, block, win, diag,
    local_sem, p_send, p_recv, f_send, f_recv, rs_send, rs_recv, ag_send, ag_recv, w_send, w_recv, d_send, d_recv,
):
    rows, features = sig.shape
    half = PANEL // 2
    chunk = features // steps
    piece = chunk // CORES
    share = rows // col_count
    start = index * PANEL
    owner, offset = start // rows, start % rows
    owner_chip, owner_core = owner // CORES, owner % CORES
    row_pos, col_pos = lax.axis_index("row"), lax.axis_index("col")
    chip, core = row_pos // CORES, row_pos % CORES
    partner = chip * CORES + 1 - core
    is_owner = row_pos == owner
    is_mate = row_pos == owner_chip * CORES + 1 - owner_core
    is_far = chip != owner_chip

    load = pltpu.make_async_copy(sig_ref, sig, local_sem.at[0])
    load.start()
    barrier = pltpu.get_barrier_semaphore()
    for step in range(1, rows_count):
        pl.semaphore_signal(barrier, inc=1, device_id={"row": (row_pos + step) % rows_count}, device_id_type=MESH)
    for step in range(1, col_count):
        pl.semaphore_signal(barrier, inc=1, device_id={"col": (col_pos + step) % col_count}, device_id_type=MESH)
    pl.semaphore_wait(barrier, rows_count + col_count - 2)

    def panel_copy(h, k, slot, target, first, width):
        lanes = pl.ds(first, width)
        return remote(
            sig_ref.at[pl.ds(offset + h * half, half), lanes],
            panel.at[pl.ds(h * half, half), lanes],
            p_send.at[h, k, slot], p_recv.at[h, k], "row", target,
        )

    def owner_copies(h, k):
        copies = []
        for other in range(rows_count):
            if other // CORES != owner_chip:
                copies.append(panel_copy(h, k, other, other, k * chunk + other % CORES * piece, piece))
        copies.append(panel_copy(h, k, owner, owner_chip * CORES + 1 - owner_core, k * chunk, chunk))
        return copies

    def forward(h, k, which):
        first = pl.multiple_of(k * chunk + which * piece, 128)
        view = panel.at[pl.ds(h * half, half), pl.ds(first, piece)]
        return remote(view, view, f_send.at[h, k], f_recv.at[h, k], "row", partner)

    def half_load(h):
        return pltpu.make_async_copy(
            sig_ref.at[pl.ds(offset + h * half, half), :], panel.at[pl.ds(h * half, half), :], local_sem.at[1 + h]
        )

    @pl.when(is_owner)
    def _():
        for h in range(2):
            for k in range(steps):
                for copy in owner_copies(h, k):
                    copy.start()
        for h in range(2):
            half_load(h).start()

    def multiply(h):
        for k in range(steps):
            if k == 0:
                @pl.when(is_owner)
                def _():
                    half_load(h).wait()

            @pl.when(is_mate)
            def _():
                panel_copy(h, k, 0, 0, k * chunk, chunk).wait_recv()

            @pl.when(is_far)
            def _():
                panel_copy(h, k, 0, 0, pl.multiple_of(k * chunk + core * piece, 128), piece).wait_recv()
                forward(h, k, core).start()
                forward(h, k, 1 - core).wait_recv()

            lanes = pl.ds(k * chunk, chunk)
            product = lax.dot_general(
                sig[:, lanes], panel[pl.ds(h * half, half), lanes], NT, preferred_element_type=jnp.float32
            )
            if k == 0:
                part[h] = product
            else:
                part[h] += product
            if h == 1 and k == steps // 2 - 1:
                gather_start(0)

    def scatter(h, step):
        peer = (col_pos + step) % col_count
        return remote(
            part.at[h, pl.ds(pl.multiple_of(peer * share, share), share)], shares.at[h, step],
            rs_send.at[h, step], rs_recv.at[h, step], "col", peer,
        )

    def gather(h, step, shift):
        mine = pl.ds(pl.multiple_of((col_pos + shift) % col_count * share, share), share)
        return remote(
            block.at[h, mine], block.at[h, mine],
            ag_send.at[h, step], ag_recv.at[h, step], "col", (col_pos + step) % col_count,
        )

    def scatter_start(h):
        for step in range(1, col_count):
            scatter(h, step).start()

    def gather_start(h):
        mine = pl.ds(pl.multiple_of(col_pos * share, share), share)
        total = part[h, mine]
        for step in range(1, col_count):
            scatter(h, step).wait_recv()
            total += shares[h, step]
        block[h, mine] = total
        for step in range(1, col_count):
            gather(h, step, 0).start()

    window_first = start + PANEL + col_pos * tile
    window_owner = window_first // rows
    window_cut = pl.ds(pl.multiple_of(window_first % rows, tile), tile)
    diagonal_cut = pl.ds(offset, PANEL)

    def window_copy(h, step):
        return remote(
            block.at[h, window_cut], win.at[h], w_send.at[h, step], w_recv.at[h],
            "row", (row_pos + step) % rows_count,
        )

    def diagonal_copy(h, step):
        return remote(
            block.at[h, diagonal_cut], diag.at[h], d_send.at[h, step], d_recv.at[h],
            "row", (row_pos + step) % rows_count,
        )

    def spread(h):
        for step in range(1, col_count):
            gather(h, step, col_count - step).wait_recv()

        @pl.when(row_pos == window_owner)
        def _():
            for step in range(1, rows_count):
                window_copy(h, step).start()

        @pl.when(is_owner)
        def _():
            for step in range(1, rows_count):
                diagonal_copy(h, step).start()

        gram_ref[:, pl.ds(h * half, half)] = block[h]

    load.wait()
    multiply(0)
    scatter_start(0)
    multiply(1)
    scatter_start(1)
    spread(0)
    gather_start(1)
    spread(1)

    for h in range(2):
        lanes = pl.ds(h * half, half)

        @pl.when(row_pos == window_owner)
        def _():
            window_ref[:, lanes] = block[h, window_cut]

        @pl.when(row_pos != window_owner)
        def _():
            window_copy(h, 1).wait_recv()
            window_ref[:, lanes] = win[h]

        @pl.when(is_owner)
        def _():
            diagonal_ref[:, lanes] = block[h, diagonal_cut]

        @pl.when(row_pos != owner)
        def _():
            diagonal_copy(h, 1).wait_recv()
            diagonal_ref[:, lanes] = diag[h]

    for h in range(2):
        for step in range(1, col_count):
            scatter(h, step).wait_send()
            gather(h, step, 0).wait_send()

        @pl.when(is_owner)
        def _():
            for k in range(steps):
                for copy in owner_copies(h, k):
                    copy.wait_send()
            for step in range(1, rows_count):
                diagonal_copy(h, step).wait_send()

        @pl.when(is_far)
        def _():
            for k in range(steps):
                forward(h, k, core).wait_send()

        @pl.when(row_pos == window_owner)
        def _():
            for step in range(1, rows_count):
                window_copy(h, step).wait_send()


def gram_columns(index, rows_count, col_count, tile, signatures):
    rows, features = signatures.shape
    steps = max(n for n in range(1, 5) if features % (n * 128 * CORES) == 0)
    half = PANEL // 2
    dma = pltpu.SemaphoreType.DMA
    vmem = pl.BlockSpec(memory_space=pltpu.VMEM)
    return pl.pallas_call(
        functools.partial(gram_kernel, index, rows_count, col_count, steps, tile),
        name=f"gram_{index}",
        out_shape=[jax.ShapeDtypeStruct((n, PANEL), jnp.float32) for n in (rows, tile, PANEL)],
        in_specs=[pl.BlockSpec(memory_space=pl.ANY)],
        out_specs=[vmem] * 3,
        scratch_shapes=[
            pltpu.VMEM((rows, features), jnp.bfloat16),
            pltpu.VMEM((PANEL, features), jnp.bfloat16),
            pltpu.VMEM((2, rows, half), jnp.float32),
            pltpu.VMEM((2, col_count, rows // col_count, half), jnp.float32),
            pltpu.VMEM((2, rows, half), jnp.float32),
            pltpu.VMEM((2, tile, half), jnp.float32),
            pltpu.VMEM((2, PANEL, half), jnp.float32),
            dma((3,)),
            dma((2, steps, rows_count)), dma((2, steps)),
            dma((2, steps)), dma((2, steps)),
            dma((2, col_count)), dma((2, col_count)),
            dma((2, col_count)), dma((2, col_count)),
            dma((2, rows_count)), dma((2,)),
            dma((2, rows_count)), dma((2,)),
        ],
        compiler_params=pltpu.CompilerParams(
            collective_id=index, has_side_effects=True, vmem_limit_bytes=40 * 1024 * 1024
        ),
    )(signatures)


def dot(a, b, dims):
    return lax.dot_general(a, b, dims, precision=lax.Precision.HIGHEST, preferred_element_type=jnp.float32)


def invert_factor(work):
    size = work.shape[0]
    row_ids = lax.broadcasted_iota(jnp.int32, (size, size), 0)
    col_ids = lax.broadcasted_iota(jnp.int32, (size, size), 1)

    def step(k, _):
        value = work[...]
        pivot_row = work[pl.ds(k, 1), :]
        at_k = col_ids == k
        column = jnp.sum(jnp.where(at_k, value, 0.0), axis=1, keepdims=True)
        pivot = jnp.sum(jnp.where(at_k[:1], pivot_row, 0.0), axis=1, keepdims=True)
        scale = jnp.where(row_ids[:, :1] > k, column / pivot, 0.0)
        base = jnp.where(at_k & (row_ids > k), 0.0, value)
        work[...] = base - scale * jnp.where(at_k[:1], 1.0, pivot_row)
        return 0

    lax.fori_loop(0, size, step, 0)
    value = work[...]
    same = row_ids == col_ids
    pivots = jnp.sum(jnp.where(same, value, 0.0), axis=1, keepdims=True)
    unit = jnp.where(row_ids > col_ids, value, jnp.where(same, 1.0, 0.0))
    return unit / jnp.sqrt(pivots)


def update_kernel(
    index_ref, ridge_ref, gram_ref, window_ref, diagonal_ref, trailing_ref, factor_ref, updated_ref, work, inverse, full
):
    rows = gram_ref.shape[0]
    share = factor_ref.shape[0]
    half = PANEL // 2
    start = index_ref[0] * PANEL
    ridge = ridge_ref[0]
    first_row = index_ref[1] * rows
    row_ids = lax.broadcasted_iota(jnp.int32, (half, half), 0)
    col_ids = lax.broadcasted_iota(jnp.int32, (half, half), 1)
    ridge_block = jnp.where(row_ids == col_ids, ridge, 0.0)
    work[...] = diagonal_ref[:half, :half] + ridge_block
    first = invert_factor(work)
    below = dot(diagonal_ref[half:, :half], first, NT)
    work[...] = diagonal_ref[half:, half:] + ridge_block - dot(below, below, NT)
    second = invert_factor(work)
    inverse[:half, :half] = first
    inverse[:half, half:] = jnp.zeros((half, half), jnp.float32)
    inverse[half:, half:] = second
    inverse[half:, :half] = -dot(second, dot(below, first, NN), NN)
    ids = first_row + lax.broadcasted_iota(jnp.int32, (rows, PANEL), 0)
    panel_ids = start + lax.broadcasted_iota(jnp.int32, (rows, PANEL), 1)
    gram = gram_ref[...] + jnp.where(ids == panel_ids, ridge, 0.0)
    full[...] = jnp.where(ids >= start, dot(gram, inverse[...], NT), 0.0)
    window = dot(window_ref[...], inverse[...], NT)
    updated_ref[...] = trailing_ref[...] - dot(full[...], window, NT)
    factor_ref[...] = full[pl.ds(pl.multiple_of(index_ref[2] * share, share), share), :]


def update(places, ridge, gram, window, diagonal, trailing, share):
    vmem = pl.BlockSpec(memory_space=pltpu.VMEM)
    smem = pl.BlockSpec(memory_space=pltpu.SMEM)
    half = PANEL // 2
    return pl.pallas_call(
        update_kernel,
        name="update",
        out_shape=[
            jax.ShapeDtypeStruct((share, PANEL), jnp.float32),
            jax.ShapeDtypeStruct(trailing.shape, jnp.float32),
        ],
        in_specs=[smem, smem] + [vmem] * 4,
        out_specs=[vmem] * 2,
        scratch_shapes=[
            pltpu.VMEM((half, half), jnp.float32),
            pltpu.VMEM((PANEL, PANEL), jnp.float32),
            pltpu.VMEM(gram.shape, jnp.float32),
        ],
        compiler_params=pltpu.CompilerParams(vmem_limit_bytes=40 * 1024 * 1024),
    )(places, ridge, gram, window, diagonal, trailing)


def solution(mesh):
    rows_count, col_count = mesh.shape["row"], mesh.shape["col"]

    def local(signatures, trailing, ridge, panel_index):
        rows, tile = signatures.shape[0], trailing.shape[1]
        panels = (rows * rows_count - tile * col_count) // PANEL
        branches = [
            functools.partial(gram_columns, index, rows_count, col_count, tile) for index in range(1, panels)
        ]
        gram, window, diagonal = lax.switch(panel_index[0] - 1, branches, signatures)
        places = jnp.stack([panel_index[0], lax.axis_index("row"), lax.axis_index("col")]).astype(jnp.int32)
        return tuple(update(places, ridge, gram, window, diagonal, trailing, rows // col_count))

    return jax.shard_map(
        local,
        mesh=mesh,
        in_specs=(P("row", "col"), P("row", "col"), P(), P()),
        out_specs=(P(("row", "col"), None), P("row", "col")),
        check_vma=False,
    )
```

```python
import functools

import jax
import jax.numpy as jnp
from jax import lax
from jax.experimental import pallas as pl
from jax.experimental.pallas import tpu as pltpu
from jax.sharding import PartitionSpec as P

PANEL = 256
CORES = 2
MESH = pl.DeviceIdType.MESH
NT = (((1,), (1,)), ((), ()))
NN = (((1,), (0,)), ((), ()))


def remote(src, dst, send, recv, axis, where):
    return pltpu.make_async_remote_copy(
        src_ref=src, dst_ref=dst, send_sem=send, recv_sem=recv, device_id={axis: where}, device_id_type=MESH
    )


def gram_kernel(
    index, rows_count, col_count, steps, tile,
    ridge_ref, sig_ref, gram_ref, window_ref, inverse_ref,
    sig, panel, part, shares, block, win, inverse, work, below,
    local_sem, p_send, p_recv, f_send, f_recv, rs_send, rs_recv, ag_send, ag_recv, w_send, w_recv, d_send, d_recv,
):
    rows, features = sig.shape
    half = PANEL // 2
    chunk = features // steps
    piece = chunk // CORES
    share = rows // col_count
    start = index * PANEL
    owner, offset = start // rows, start % rows
    owner_chip, owner_core = owner // CORES, owner % CORES
    row_pos, col_pos = lax.axis_index("row"), lax.axis_index("col")
    chip, core = row_pos // CORES, row_pos % CORES
    partner = chip * CORES + 1 - core
    is_owner = row_pos == owner
    is_mate = row_pos == owner_chip * CORES + 1 - owner_core
    is_far = chip != owner_chip

    load = pltpu.make_async_copy(sig_ref, sig, local_sem.at[0])
    load.start()
    barrier = pltpu.get_barrier_semaphore()
    for step in range(1, rows_count):
        pl.semaphore_signal(barrier, inc=1, device_id={"row": (row_pos + step) % rows_count}, device_id_type=MESH)
    for step in range(1, col_count):
        pl.semaphore_signal(barrier, inc=1, device_id={"col": (col_pos + step) % col_count}, device_id_type=MESH)
    pl.semaphore_wait(barrier, rows_count + col_count - 2)

    def panel_copy(h, k, slot, target, first, width):
        lanes = pl.ds(first, width)
        return remote(
            sig_ref.at[pl.ds(offset + h * half, half), lanes],
            panel.at[pl.ds(h * half, half), lanes],
            p_send.at[h, k, slot], p_recv.at[h, k], "row", target,
        )

    def owner_copies(h, k):
        copies = []
        for other in range(rows_count):
            if other // CORES != owner_chip:
                copies.append(panel_copy(h, k, other, other, k * chunk + other % CORES * piece, piece))
        copies.append(panel_copy(h, k, owner, owner_chip * CORES + 1 - owner_core, k * chunk, chunk))
        return copies

    def forward(h, k, which):
        first = pl.multiple_of(k * chunk + which * piece, 128)
        view = panel.at[pl.ds(h * half, half), pl.ds(first, piece)]
        return remote(view, view, f_send.at[h, k], f_recv.at[h, k], "row", partner)

    def half_load(h):
        return pltpu.make_async_copy(
            sig_ref.at[pl.ds(offset + h * half, half), :], panel.at[pl.ds(h * half, half), :], local_sem.at[1 + h]
        )

    @pl.when(is_owner)
    def _():
        for h in range(2):
            for k in range(steps):
                for copy in owner_copies(h, k):
                    copy.start()
        for h in range(2):
            half_load(h).start()

    def multiply(h):
        for k in range(steps):
            if k == 0:
                @pl.when(is_owner)
                def _():
                    half_load(h).wait()

            @pl.when(is_mate)
            def _():
                panel_copy(h, k, 0, 0, k * chunk, chunk).wait_recv()

            @pl.when(is_far)
            def _():
                panel_copy(h, k, 0, 0, pl.multiple_of(k * chunk + core * piece, 128), piece).wait_recv()
                forward(h, k, core).start()
                forward(h, k, 1 - core).wait_recv()

            lanes = pl.ds(k * chunk, chunk)
            product = lax.dot_general(
                sig[:, lanes], panel[pl.ds(h * half, half), lanes], NT, preferred_element_type=jnp.float32
            )
            if k == 0:
                part[h] = product
            else:
                part[h] += product
            if h == 1 and k == steps // 2 - 1:
                gather_start(0)

    def scatter(h, step):
        peer = (col_pos + step) % col_count
        return remote(
            part.at[h, pl.ds(pl.multiple_of(peer * share, share), share)], shares.at[h, step],
            rs_send.at[h, step], rs_recv.at[h, step], "col", peer,
        )

    def gather(h, step, shift):
        mine = pl.ds(pl.multiple_of((col_pos + shift) % col_count * share, share), share)
        return remote(
            block.at[h, mine], block.at[h, mine],
            ag_send.at[h, step], ag_recv.at[h, step], "col", (col_pos + step) % col_count,
        )

    def scatter_start(h):
        for step in range(1, col_count):
            scatter(h, step).start()

    def gather_start(h):
        mine = pl.ds(pl.multiple_of(col_pos * share, share), share)
        total = part[h, mine]
        for step in range(1, col_count):
            scatter(h, step).wait_recv()
            total += shares[h, step]
        block[h, mine] = total
        for step in range(1, col_count):
            gather(h, step, 0).start()

    window_first = start + PANEL + col_pos * tile
    window_owner = window_first // rows
    window_cut = pl.ds(pl.multiple_of(window_first % rows, tile), tile)

    def window_copy(h, step):
        return remote(
            block.at[h, window_cut], win.at[h], w_send.at[h, step], w_recv.at[h],
            "row", (row_pos + step) % rows_count,
        )

    def inverse_copy(h, step):
        view = inverse.at[h, pl.ds(h * half, PANEL - h * half)]
        return remote(
            view, view, d_send.at[h, step], d_recv.at[h], "row", (row_pos + step) % rows_count,
        )

    row_ids = lax.broadcasted_iota(jnp.int32, (half, half), 0)
    col_ids = lax.broadcasted_iota(jnp.int32, (half, half), 1)
    upper, lower = pl.ds(offset, half), pl.ds(offset + half, half)

    def invert_first():
        work[...] = block[0, upper] + jnp.where(row_ids == col_ids, ridge_ref[0], 0.0)
        first = invert_factor(work)
        inverse[0, :half] = first
        below[...] = dot(block[0, lower], first, NT)

    def invert_second():
        ridge_block = jnp.where(row_ids == col_ids, ridge_ref[0], 0.0)
        work[...] = block[1, lower] + ridge_block - dot(below[...], below[...], NT)
        second = invert_factor(work)
        inverse[1, half:] = second
        inverse[0, half:] = -dot(second, dot(below[...], inverse[0, :half], NN), NN)

    def spread(h):
        for step in range(1, col_count):
            gather(h, step, col_count - step).wait_recv()

        @pl.when(row_pos == window_owner)
        def _():
            for step in range(1, rows_count):
                window_copy(h, step).start()

        gram_ref[:, pl.ds(h * half, half)] = block[h]

    load.wait()
    multiply(0)
    scatter_start(0)
    multiply(1)
    scatter_start(1)
    spread(0)
    gather_start(1)
    pl.when(is_owner)(invert_first)
    spread(1)

    @pl.when(is_owner)
    def _():
        invert_second()
        for h in range(2):
            for step in range(1, rows_count):
                inverse_copy(h, step).start()

    for h in range(2):
        lanes = pl.ds(h * half, half)

        @pl.when(row_pos == window_owner)
        def _():
            window_ref[:, lanes] = block[h, window_cut]

        @pl.when(row_pos != window_owner)
        def _():
            window_copy(h, 1).wait_recv()
            window_ref[:, lanes] = win[h]

        @pl.when(row_pos != owner)
        def _():
            inverse_copy(h, 1).wait_recv()

    inverse_ref[:, :half] = inverse[0]
    inverse_ref[half:, half:] = inverse[1, half:]
    inverse_ref[:half, half:] = jnp.zeros((half, half), jnp.float32)

    for h in range(2):
        for step in range(1, col_count):
            scatter(h, step).wait_send()
            gather(h, step, 0).wait_send()

        @pl.when(is_owner)
        def _():
            for k in range(steps):
                for copy in owner_copies(h, k):
                    copy.wait_send()
            for step in range(1, rows_count):
                inverse_copy(h, step).wait_send()

        @pl.when(is_far)
        def _():
            for k in range(steps):
                forward(h, k, core).wait_send()

        @pl.when(row_pos == window_owner)
        def _():
            for step in range(1, rows_count):
                window_copy(h, step).wait_send()


def gram_columns(index, rows_count, col_count, tile, ridge, signatures):
    rows, features = signatures.shape
    steps = max(n for n in range(1, 5) if features % (n * 128 * CORES) == 0)
    half = PANEL // 2
    dma = pltpu.SemaphoreType.DMA
    vmem = pl.BlockSpec(memory_space=pltpu.VMEM)
    return pl.pallas_call(
        functools.partial(gram_kernel, index, rows_count, col_count, steps, tile),
        name=f"gram_{index}",
        out_shape=[jax.ShapeDtypeStruct((n, PANEL), jnp.float32) for n in (rows, tile, PANEL)],
        in_specs=[pl.BlockSpec(memory_space=pltpu.SMEM), pl.BlockSpec(memory_space=pl.ANY)],
        out_specs=[vmem] * 3,
        scratch_shapes=[
            pltpu.VMEM((rows, features), jnp.bfloat16),
            pltpu.VMEM((PANEL, features), jnp.bfloat16),
            pltpu.VMEM((2, rows, half), jnp.float32),
            pltpu.VMEM((2, col_count, rows // col_count, half), jnp.float32),
            pltpu.VMEM((2, rows, half), jnp.float32),
            pltpu.VMEM((2, tile, half), jnp.float32),
            pltpu.VMEM((2, PANEL, half), jnp.float32),
            pltpu.VMEM((half, half), jnp.float32),
            pltpu.VMEM((half, half), jnp.float32),
            dma((3,)),
            dma((2, steps, rows_count)), dma((2, steps)),
            dma((2, steps)), dma((2, steps)),
            dma((2, col_count)), dma((2, col_count)),
            dma((2, col_count)), dma((2, col_count)),
            dma((2, rows_count)), dma((2,)),
            dma((2, rows_count)), dma((2,)),
        ],
        compiler_params=pltpu.CompilerParams(
            collective_id=index, has_side_effects=True, vmem_limit_bytes=40 * 1024 * 1024
        ),
    )(ridge, signatures)


def dot(a, b, dims):
    return lax.dot_general(a, b, dims, precision=lax.Precision.HIGHEST, preferred_element_type=jnp.float32)


def invert_factor(work):
    size = work.shape[0]
    segment = size // 4

    def pick(mask, value):
        return jnp.sum(jnp.where(mask, value, 0.0), axis=1, keepdims=True)

    for top in range(0, size, segment):
        active = size - top
        rows = top + lax.broadcasted_iota(jnp.int32, (active, 1), 0)
        lanes = lax.broadcasted_iota(jnp.int32, (active, size), 1)
        lane = lax.broadcasted_iota(jnp.int32, (1, size), 1)

        def pair(i, _):
            k = top + 2 * i
            value = work[top:, :]
            row_0, row_1 = work[pl.ds(k, 1), :], work[pl.ds(k + 1, 1), :]
            at_0, at_1 = lane == k, lane == k + 1
            column_0 = pick(lanes == k, value)
            column_1 = pick(lanes == k + 1, value)
            cross = pick(at_1, row_0)
            over_0 = 1.0 / pick(at_0, row_0)
            ratio = pick(at_0, row_1) * over_0
            over_1 = 1.0 / (pick(at_1, row_1) - ratio * cross)
            unit_0 = jnp.where(at_0, 1.0, row_0)
            next_1 = jnp.where(at_0, 0.0, row_1) - ratio * unit_0
            later = rows > k + 1
            scale_0 = jnp.where(later, column_0 * over_0, 0.0)
            scale_1 = jnp.where(later, (column_1 - scale_0 * cross) * over_1, 0.0)
            base = jnp.where(later & ((lanes == k) | (lanes == k + 1)), 0.0, value)
            work[top:, :] = (
                base - scale_0 * jnp.where(at_1, 0.0, unit_0) - scale_1 * jnp.where(at_1, 1.0, next_1)
            )
            work[pl.ds(k + 1, 1), :] = next_1
            return 0

        lax.fori_loop(0, segment // 2, pair, 0)
    row_ids = lax.broadcasted_iota(jnp.int32, (size, size), 0)
    col_ids = lax.broadcasted_iota(jnp.int32, (size, size), 1)
    value = work[...]
    same = row_ids == col_ids
    unit = jnp.where(row_ids > col_ids, value, jnp.where(same, 1.0, 0.0))
    return unit / jnp.sqrt(pick(same, value))


def update_kernel(
    index_ref, ridge_ref, gram_ref, window_ref, inverse_ref, trailing_ref, factor_ref, updated_ref, full
):
    rows = gram_ref.shape[0]
    share = factor_ref.shape[0]
    start = index_ref[0] * PANEL
    ridge = ridge_ref[0]
    first_row = index_ref[1] * rows
    ids = first_row + lax.broadcasted_iota(jnp.int32, (rows, PANEL), 0)
    panel_ids = start + lax.broadcasted_iota(jnp.int32, (rows, PANEL), 1)
    gram = gram_ref[...] + jnp.where(ids == panel_ids, ridge, 0.0)
    full[...] = jnp.where(ids >= start, dot(gram, inverse_ref[...], NT), 0.0)
    window = dot(window_ref[...], inverse_ref[...], NT)
    updated_ref[...] = trailing_ref[...] - dot(full[...], window, NT)
    factor_ref[...] = full[pl.ds(pl.multiple_of(index_ref[2] * share, share), share), :]


def update(places, ridge, gram, window, inverse, trailing, share):
    vmem = pl.BlockSpec(memory_space=pltpu.VMEM)
    smem = pl.BlockSpec(memory_space=pltpu.SMEM)
    return pl.pallas_call(
        update_kernel,
        name="update",
        out_shape=[
            jax.ShapeDtypeStruct((share, PANEL), jnp.float32),
            jax.ShapeDtypeStruct(trailing.shape, jnp.float32),
        ],
        in_specs=[smem, smem] + [vmem] * 4,
        out_specs=[vmem] * 2,
        scratch_shapes=[pltpu.VMEM(gram.shape, jnp.float32)],
        compiler_params=pltpu.CompilerParams(vmem_limit_bytes=40 * 1024 * 1024),
    )(places, ridge, gram, window, inverse, trailing)


def solution(mesh):
    rows_count, col_count = mesh.shape["row"], mesh.shape["col"]

    def local(signatures, trailing, ridge, panel_index):
        rows, tile = signatures.shape[0], trailing.shape[1]
        panels = (rows * rows_count - tile * col_count) // PANEL
        branches = [
            functools.partial(gram_columns, index, rows_count, col_count, tile) for index in range(1, panels)
        ]
        gram, window, inverse = lax.switch(panel_index[0] - 1, branches, ridge, signatures)
        places = jnp.stack([panel_index[0], lax.axis_index("row"), lax.axis_index("col")]).astype(jnp.int32)
        return tuple(update(places, ridge, gram, window, inverse, trailing, rows // col_count))

    return jax.shard_map(
        local,
        mesh=mesh,
        in_specs=(P("row", "col"), P("row", "col"), P(), P()),
        out_specs=(P(("row", "col"), None), P("row", "col")),
        check_vma=False,
    )
```

```python
import functools

import jax
import jax.numpy as jnp
from jax import lax
from jax.experimental import pallas as pl
from jax.experimental.pallas import tpu as pltpu
from jax.sharding import PartitionSpec as P

PANEL = 256
CORES = 2
MESH = pl.DeviceIdType.MESH
NT = (((1,), (1,)), ((), ()))
NN = (((1,), (0,)), ((), ()))


def remote(src, dst, send, recv, axis, where):
    return pltpu.make_async_remote_copy(
        src_ref=src, dst_ref=dst, send_sem=send, recv_sem=recv, device_id={axis: where}, device_id_type=MESH
    )


def gram_kernel(
    index, rows_count, col_count, steps, tile,
    ridge_ref, sig_ref, gram_ref, window_ref, inverse_ref,
    sig, panel, part, shares, block, win, inverse, work, below,
    local_sem, p_send, p_recv, f_send, f_recv, rs_send, rs_recv, ag_send, ag_recv, w_send, w_recv, d_send, d_recv,
):
    rows, features = sig.shape
    half = PANEL // 2
    chunk = features // steps
    piece = chunk // CORES
    share = rows // col_count
    start = index * PANEL
    owner, offset = start // rows, start % rows
    owner_chip, owner_core = owner // CORES, owner % CORES
    row_pos, col_pos = lax.axis_index("row"), lax.axis_index("col")
    chip, core = row_pos // CORES, row_pos % CORES
    partner = chip * CORES + 1 - core
    is_owner = row_pos == owner
    is_mate = row_pos == owner_chip * CORES + 1 - owner_core
    is_far = chip != owner_chip

    load = pltpu.make_async_copy(sig_ref, sig, local_sem.at[0])
    load.start()
    barrier = pltpu.get_barrier_semaphore()
    for step in range(1, rows_count):
        pl.semaphore_signal(barrier, inc=1, device_id={"row": (row_pos + step) % rows_count}, device_id_type=MESH)
    for step in range(1, col_count):
        pl.semaphore_signal(barrier, inc=1, device_id={"col": (col_pos + step) % col_count}, device_id_type=MESH)
    window_first = start + PANEL + col_pos * tile
    window_owner = window_first // rows
    window_cut = pl.ds(pl.multiple_of(window_first % rows, tile), tile)
    slots = tile // share

    @pl.when(row_pos != window_owner)
    def _():
        for slot in range(slots):
            pl.semaphore_signal(
                barrier, inc=1, device_id={"row": window_owner, "col": window_first % rows // share + slot},
                device_id_type=MESH,
            )

    share_first = row_pos * rows + col_pos * share - (start + PANEL)
    in_window = (share_first >= 0) & (share_first < tile * col_count)
    share_place = jnp.maximum(share_first, 0)
    neighbours = rows_count + col_count - 2
    pl.semaphore_wait(barrier, jnp.where(in_window, neighbours + rows_count - 1, neighbours))

    def panel_copy(h, k, slot, target, first, width):
        lanes = pl.ds(first, width)
        return remote(
            sig_ref.at[pl.ds(offset + h * half, half), lanes],
            panel.at[pl.ds(h * half, half), lanes],
            p_send.at[h, k, slot], p_recv.at[h, k], "row", target,
        )

    def owner_copies(h, k):
        copies = []
        for other in range(rows_count):
            if other // CORES != owner_chip:
                copies.append(panel_copy(h, k, other, other, k * chunk + other % CORES * piece, piece))
        copies.append(panel_copy(h, k, owner, owner_chip * CORES + 1 - owner_core, k * chunk, chunk))
        return copies

    def forward(h, k, which):
        first = pl.multiple_of(k * chunk + which * piece, 128)
        view = panel.at[pl.ds(h * half, half), pl.ds(first, piece)]
        return remote(view, view, f_send.at[h, k], f_recv.at[h, k], "row", partner)

    def half_load(h):
        return pltpu.make_async_copy(
            sig_ref.at[pl.ds(offset + h * half, half), :], panel.at[pl.ds(h * half, half), :], local_sem.at[1 + h]
        )

    @pl.when(is_owner)
    def _():
        for h in range(2):
            for k in range(steps):
                for copy in owner_copies(h, k):
                    copy.start()
        for h in range(2):
            half_load(h).start()

    def multiply(h):
        for k in range(steps):
            if k == 0:
                @pl.when(is_owner)
                def _():
                    half_load(h).wait()

            @pl.when(is_mate)
            def _():
                panel_copy(h, k, 0, 0, k * chunk, chunk).wait_recv()

            @pl.when(is_far)
            def _():
                panel_copy(h, k, 0, 0, pl.multiple_of(k * chunk + core * piece, 128), piece).wait_recv()
                forward(h, k, core).start()
                forward(h, k, 1 - core).wait_recv()

            lanes = pl.ds(k * chunk, chunk)
            product = lax.dot_general(
                sig[:, lanes], panel[pl.ds(h * half, half), lanes], NT, preferred_element_type=jnp.float32
            )
            if k == 0:
                part[h] = product
            else:
                part[h] += product
            if h == 1 and k == steps // 2 - 1:
                gather_start(0)

    def scatter(h, step):
        peer = (col_pos + step) % col_count
        return remote(
            part.at[h, pl.ds(pl.multiple_of(peer * share, share), share)], shares.at[h, step],
            rs_send.at[h, step], rs_recv.at[h, step], "col", peer,
        )

    def gather(h, step, shift):
        mine = pl.ds(pl.multiple_of((col_pos + shift) % col_count * share, share), share)
        return remote(
            block.at[h, mine], block.at[h, mine],
            ag_send.at[h, step], ag_recv.at[h, step], "col", (col_pos + step) % col_count,
        )

    def window_copy(h, step):
        mine = pl.ds(pl.multiple_of(col_pos * share, share), share)
        slot = share_place % tile // share
        return pltpu.make_async_remote_copy(
            src_ref=block.at[h, mine],
            dst_ref=win.at[h, pl.ds(pl.multiple_of(slot * share, share), share)],
            send_sem=w_send.at[h, step],
            recv_sem=w_recv.at[h, slot],
            device_id={"row": (row_pos + step) % rows_count, "col": share_place // tile},
            device_id_type=MESH,
        )

    def window_wait(h):
        for slot in range(slots):
            view = win.at[h, pl.ds(slot * share, share)]
            remote(view, view, w_send.at[h, 1], w_recv.at[h, slot], "row", (row_pos + 1) % rows_count).wait_recv()

    def scatter_start(h):
        for step in range(1, col_count):
            scatter(h, step).start()

    def gather_start(h):
        mine = pl.ds(pl.multiple_of(col_pos * share, share), share)
        total = part[h, mine]
        for step in range(1, col_count):
            scatter(h, step).wait_recv()
            total += shares[h, step]
        block[h, mine] = total

        @pl.when(in_window)
        def _():
            for step in range(1, rows_count):
                window_copy(h, step).start()

        for step in range(1, col_count):
            gather(h, step, 0).start()

    def inverse_copy(h, step):
        view = inverse.at[h, pl.ds(h * half, PANEL - h * half)]
        return remote(
            view, view, d_send.at[h, step], d_recv.at[h], "row", (row_pos + step) % rows_count,
        )

    row_ids = lax.broadcasted_iota(jnp.int32, (half, half), 0)
    col_ids = lax.broadcasted_iota(jnp.int32, (half, half), 1)
    upper, lower = pl.ds(offset, half), pl.ds(offset + half, half)

    def invert_first():
        work[...] = block[0, upper] + jnp.where(row_ids == col_ids, ridge_ref[0], 0.0)
        first = invert_factor(work)
        inverse[0, :half] = first
        below[...] = dot(block[0, lower], first, NT)

    def invert_second():
        ridge_block = jnp.where(row_ids == col_ids, ridge_ref[0], 0.0)
        work[...] = block[1, lower] + ridge_block - dot(below[...], below[...], NT)
        second = invert_factor(work)
        inverse[1, half:] = second
        inverse[0, half:] = -dot(second, dot(below[...], inverse[0, :half], NN), NN)

    def spread(h):
        for step in range(1, col_count):
            gather(h, step, col_count - step).wait_recv()

        gram_ref[:, pl.ds(h * half, half)] = block[h]

    load.wait()
    multiply(0)
    scatter_start(0)
    multiply(1)
    scatter_start(1)
    spread(0)
    gather_start(1)
    pl.when(is_owner)(invert_first)
    spread(1)

    @pl.when(is_owner)
    def _():
        invert_second()
        for h in range(2):
            for step in range(1, rows_count):
                inverse_copy(h, step).start()

    for h in range(2):
        lanes = pl.ds(h * half, half)

        @pl.when(row_pos == window_owner)
        def _():
            window_ref[:, lanes] = block[h, window_cut]

        @pl.when(row_pos != window_owner)
        def _():
            window_wait(h)
            window_ref[:, lanes] = win[h]

        @pl.when(row_pos != owner)
        def _():
            inverse_copy(h, 1).wait_recv()

    inverse_ref[:, :half] = inverse[0]
    inverse_ref[half:, half:] = inverse[1, half:]
    inverse_ref[:half, half:] = jnp.zeros((half, half), jnp.float32)

    for h in range(2):
        for step in range(1, col_count):
            scatter(h, step).wait_send()
            gather(h, step, 0).wait_send()

        @pl.when(is_owner)
        def _():
            for k in range(steps):
                for copy in owner_copies(h, k):
                    copy.wait_send()
            for step in range(1, rows_count):
                inverse_copy(h, step).wait_send()

        @pl.when(is_far)
        def _():
            for k in range(steps):
                forward(h, k, core).wait_send()

        @pl.when(in_window)
        def _():
            for step in range(1, rows_count):
                window_copy(h, step).wait_send()


def gram_columns(index, rows_count, col_count, tile, ridge, signatures):
    rows, features = signatures.shape
    steps = max(n for n in range(1, 5) if features % (n * 128 * CORES) == 0)
    half = PANEL // 2
    dma = pltpu.SemaphoreType.DMA
    vmem = pl.BlockSpec(memory_space=pltpu.VMEM)
    return pl.pallas_call(
        functools.partial(gram_kernel, index, rows_count, col_count, steps, tile),
        name=f"gram_{index}",
        out_shape=[jax.ShapeDtypeStruct((n, PANEL), jnp.float32) for n in (rows, tile, PANEL)],
        in_specs=[pl.BlockSpec(memory_space=pltpu.SMEM), pl.BlockSpec(memory_space=pl.ANY)],
        out_specs=[vmem] * 3,
        scratch_shapes=[
            pltpu.VMEM((rows, features), jnp.bfloat16),
            pltpu.VMEM((PANEL, features), jnp.bfloat16),
            pltpu.VMEM((2, rows, half), jnp.float32),
            pltpu.VMEM((2, col_count, rows // col_count, half), jnp.float32),
            pltpu.VMEM((2, rows, half), jnp.float32),
            pltpu.VMEM((2, tile, half), jnp.float32),
            pltpu.VMEM((2, PANEL, half), jnp.float32),
            pltpu.VMEM((half, half), jnp.float32),
            pltpu.VMEM((half, half), jnp.float32),
            dma((3,)),
            dma((2, steps, rows_count)), dma((2, steps)),
            dma((2, steps)), dma((2, steps)),
            dma((2, col_count)), dma((2, col_count)),
            dma((2, col_count)), dma((2, col_count)),
            dma((2, rows_count)), dma((2, tile * col_count // rows)),
            dma((2, rows_count)), dma((2,)),
        ],
        compiler_params=pltpu.CompilerParams(
            collective_id=index, has_side_effects=True, vmem_limit_bytes=40 * 1024 * 1024
        ),
    )(ridge, signatures)


def dot(a, b, dims):
    return lax.dot_general(a, b, dims, precision=lax.Precision.HIGHEST, preferred_element_type=jnp.float32)


def invert_factor(work):
    size = work.shape[0]
    segment = size // 4

    def pick(mask, value):
        return jnp.sum(jnp.where(mask, value, 0.0), axis=1, keepdims=True)

    for top in range(0, size, segment):
        active = size - top
        rows = top + lax.broadcasted_iota(jnp.int32, (active, 1), 0)
        lanes = lax.broadcasted_iota(jnp.int32, (active, size), 1)
        lane = lax.broadcasted_iota(jnp.int32, (1, size), 1)

        def pair(i, _):
            k = top + 2 * i
            value = work[top:, :]
            row_0, row_1 = work[pl.ds(k, 1), :], work[pl.ds(k + 1, 1), :]
            at_0, at_1 = lane == k, lane == k + 1
            column_0 = pick(lanes == k, value)
            column_1 = pick(lanes == k + 1, value)
            cross = pick(at_1, row_0)
            over_0 = 1.0 / pick(at_0, row_0)
            ratio = pick(at_0, row_1) * over_0
            over_1 = 1.0 / (pick(at_1, row_1) - ratio * cross)
            unit_0 = jnp.where(at_0, 1.0, row_0)
            next_1 = jnp.where(at_0, 0.0, row_1) - ratio * unit_0
            later = rows > k + 1
            scale_0 = jnp.where(later, column_0 * over_0, 0.0)
            scale_1 = jnp.where(later, (column_1 - scale_0 * cross) * over_1, 0.0)
            base = jnp.where(later & ((lanes == k) | (lanes == k + 1)), 0.0, value)
            work[top:, :] = (
                base - scale_0 * jnp.where(at_1, 0.0, unit_0) - scale_1 * jnp.where(at_1, 1.0, next_1)
            )
            work[pl.ds(k + 1, 1), :] = next_1
            return 0

        lax.fori_loop(0, segment // 2, pair, 0)
    row_ids = lax.broadcasted_iota(jnp.int32, (size, size), 0)
    col_ids = lax.broadcasted_iota(jnp.int32, (size, size), 1)
    value = work[...]
    same = row_ids == col_ids
    unit = jnp.where(row_ids > col_ids, value, jnp.where(same, 1.0, 0.0))
    return unit / jnp.sqrt(pick(same, value))


def update_kernel(
    index_ref, ridge_ref, gram_ref, window_ref, inverse_ref, trailing_ref, factor_ref, updated_ref, full
):
    rows = gram_ref.shape[0]
    share = factor_ref.shape[0]
    start = index_ref[0] * PANEL
    ridge = ridge_ref[0]
    first_row = index_ref[1] * rows
    ids = first_row + lax.broadcasted_iota(jnp.int32, (rows, PANEL), 0)
    panel_ids = start + lax.broadcasted_iota(jnp.int32, (rows, PANEL), 1)
    gram = gram_ref[...] + jnp.where(ids == panel_ids, ridge, 0.0)
    full[...] = jnp.where(ids >= start, dot(gram, inverse_ref[...], NT), 0.0)
    window = dot(window_ref[...], inverse_ref[...], NT)
    updated_ref[...] = trailing_ref[...] - dot(full[...], window, NT)
    factor_ref[...] = full[pl.ds(pl.multiple_of(index_ref[2] * share, share), share), :]


def update(places, ridge, gram, window, inverse, trailing, share):
    vmem = pl.BlockSpec(memory_space=pltpu.VMEM)
    smem = pl.BlockSpec(memory_space=pltpu.SMEM)
    return pl.pallas_call(
        update_kernel,
        name="update",
        out_shape=[
            jax.ShapeDtypeStruct((share, PANEL), jnp.float32),
            jax.ShapeDtypeStruct(trailing.shape, jnp.float32),
        ],
        in_specs=[smem, smem] + [vmem] * 4,
        out_specs=[vmem] * 2,
        scratch_shapes=[pltpu.VMEM(gram.shape, jnp.float32)],
        compiler_params=pltpu.CompilerParams(vmem_limit_bytes=40 * 1024 * 1024),
    )(places, ridge, gram, window, inverse, trailing)


def solution(mesh):
    rows_count, col_count = mesh.shape["row"], mesh.shape["col"]

    def local(signatures, trailing, ridge, panel_index):
        rows, tile = signatures.shape[0], trailing.shape[1]
        panels = (rows * rows_count - tile * col_count) // PANEL
        branches = [
            functools.partial(gram_columns, index, rows_count, col_count, tile) for index in range(1, panels)
        ]
        gram, window, inverse = lax.switch(panel_index[0] - 1, branches, ridge, signatures)
        places = jnp.stack([panel_index[0], lax.axis_index("row"), lax.axis_index("col")]).astype(jnp.int32)
        return tuple(update(places, ridge, gram, window, inverse, trailing, rows // col_count))

    return jax.shard_map(
        local,
        mesh=mesh,
        in_specs=(P("row", "col"), P("row", "col"), P(), P()),
        out_specs=(P(("row", "col"), None), P("row", "col")),
        check_vma=False,
    )
```

```python
import functools

import jax
import jax.numpy as jnp
from jax import lax
from jax.experimental import pallas as pl
from jax.experimental.pallas import tpu as pltpu
from jax.sharding import PartitionSpec as P

PANEL = 256
CORES = 2
MESH = pl.DeviceIdType.MESH
NT = (((1,), (1,)), ((), ()))
NN = (((1,), (0,)), ((), ()))


def remote(src, dst, send, recv, axis, where):
    return pltpu.make_async_remote_copy(
        src_ref=src, dst_ref=dst, send_sem=send, recv_sem=recv, device_id={axis: where}, device_id_type=MESH
    )


def gram_kernel(
    index, rows_count, col_count, steps, tile,
    ridge_ref, sig_ref, gram_ref, window_ref, inverse_ref,
    sig, panel, part, shares, block, win, inverse, work, below,
    local_sem, p_send, p_recv, f_send, f_recv, rs_send, rs_recv, ag_send, ag_recv, w_send, w_recv, d_send, d_recv,
):
    rows, features = sig.shape
    half = PANEL // 2
    chunk = features // steps
    piece = chunk // CORES
    share = rows // col_count
    start = index * PANEL
    owner, offset = start // rows, start % rows
    owner_chip, owner_core = owner // CORES, owner % CORES
    row_pos, col_pos = lax.axis_index("row"), lax.axis_index("col")
    chip, core = row_pos // CORES, row_pos % CORES
    partner = chip * CORES + 1 - core
    is_owner = row_pos == owner
    is_mate = row_pos == owner_chip * CORES + 1 - owner_core
    is_far = chip != owner_chip

    load = pltpu.make_async_copy(sig_ref, sig, local_sem.at[0])
    load.start()
    barrier = pltpu.get_barrier_semaphore()
    for step in range(1, rows_count):
        pl.semaphore_signal(barrier, inc=1, device_id={"row": (row_pos + step) % rows_count}, device_id_type=MESH)
    for step in range(1, col_count):
        pl.semaphore_signal(barrier, inc=1, device_id={"col": (col_pos + step) % col_count}, device_id_type=MESH)
    window_first = start + PANEL + col_pos * tile
    window_owner = window_first // rows
    window_cut = pl.ds(pl.multiple_of(window_first % rows, tile), tile)
    slots = tile // share

    @pl.when(row_pos != window_owner)
    def _():
        for slot in range(slots):
            pl.semaphore_signal(
                barrier, inc=1, device_id={"row": window_owner, "col": window_first % rows // share + slot},
                device_id_type=MESH,
            )

    share_first = row_pos * rows + col_pos * share - (start + PANEL)
    in_window = (share_first >= 0) & (share_first < tile * col_count)
    share_place = jnp.maximum(share_first, 0)
    neighbours = rows_count + col_count - 2
    pl.semaphore_wait(barrier, jnp.where(in_window, neighbours + rows_count - 1, neighbours))

    def panel_copy(h, k, slot, target, first, width):
        lanes = pl.ds(first, width)
        return remote(
            sig_ref.at[pl.ds(offset + h * half, half), lanes],
            panel.at[pl.ds(h * half, half), lanes],
            p_send.at[h, k, slot], p_recv.at[h, k], "row", target,
        )

    def owner_copies(h, k):
        copies = []
        for other in range(rows_count):
            if other // CORES != owner_chip:
                copies.append(panel_copy(h, k, other, other, k * chunk + other % CORES * piece, piece))
        copies.append(panel_copy(h, k, owner, owner_chip * CORES + 1 - owner_core, k * chunk, chunk))
        return copies

    def forward(h, k, which):
        first = pl.multiple_of(k * chunk + which * piece, 128)
        view = panel.at[pl.ds(h * half, half), pl.ds(first, piece)]
        return remote(view, view, f_send.at[h, k], f_recv.at[h, k], "row", partner)

    def half_load(h):
        return pltpu.make_async_copy(
            sig_ref.at[pl.ds(offset + h * half, half), :], panel.at[pl.ds(h * half, half), :], local_sem.at[1 + h]
        )

    @pl.when(is_owner)
    def _():
        for h in range(2):
            for k in range(steps):
                for copy in owner_copies(h, k):
                    copy.start()
        for h in range(2):
            half_load(h).start()

    def multiply(h):
        for k in range(steps):
            if k == 0:
                @pl.when(is_owner)
                def _():
                    half_load(h).wait()

            @pl.when(is_mate)
            def _():
                panel_copy(h, k, 0, 0, k * chunk, chunk).wait_recv()

            @pl.when(is_far)
            def _():
                panel_copy(h, k, 0, 0, pl.multiple_of(k * chunk + core * piece, 128), piece).wait_recv()
                forward(h, k, core).start()
                forward(h, k, 1 - core).wait_recv()

            lanes = pl.ds(k * chunk, chunk)
            product = lax.dot_general(
                sig[:, lanes], panel[pl.ds(h * half, half), lanes], NT, preferred_element_type=jnp.float32
            )
            if k == 0:
                part[h] = product
            else:
                part[h] += product
            if h == 1 and k == steps // 2 - 1:
                gather_start(0)

    def scatter(h, step):
        peer = (col_pos + step) % col_count
        return remote(
            part.at[h, pl.ds(pl.multiple_of(peer * share, share), share)], shares.at[h, step],
            rs_send.at[h, step], rs_recv.at[h, step], "col", peer,
        )

    def gather(h, step, shift):
        mine = pl.ds(pl.multiple_of((col_pos + shift) % col_count * share, share), share)
        return remote(
            block.at[h, mine], block.at[h, mine],
            ag_send.at[h, step], ag_recv.at[h, step], "col", (col_pos + step) % col_count,
        )

    def window_copy(h, step):
        mine = pl.ds(pl.multiple_of(col_pos * share, share), share)
        slot = share_place % tile // share
        return pltpu.make_async_remote_copy(
            src_ref=block.at[h, mine],
            dst_ref=win.at[h, pl.ds(pl.multiple_of(slot * share, share), share)],
            send_sem=w_send.at[h, step],
            recv_sem=w_recv.at[h, slot],
            device_id={"row": (row_pos + step) % rows_count, "col": share_place // tile},
            device_id_type=MESH,
        )

    def window_wait(h):
        for slot in range(slots):
            view = win.at[h, pl.ds(slot * share, share)]
            remote(view, view, w_send.at[h, 1], w_recv.at[h, slot], "row", (row_pos + 1) % rows_count).wait_recv()

    def scatter_start(h):
        for step in range(1, col_count):
            scatter(h, step).start()

    def gather_start(h):
        mine = pl.ds(pl.multiple_of(col_pos * share, share), share)
        total = part[h, mine]
        for step in range(1, col_count):
            scatter(h, step).wait_recv()
            total += shares[h, step]
        block[h, mine] = total

        @pl.when(in_window)
        def _():
            for step in range(1, rows_count):
                window_copy(h, step).start()

        for step in range(1, col_count):
            gather(h, step, 0).start()

    def inverse_copy(h, step):
        view = inverse.at[h, pl.ds(h * half, PANEL - h * half)]
        return remote(
            view, view, d_send.at[h, step], d_recv.at[h], "row", (row_pos + step) % rows_count,
        )

    row_ids = lax.broadcasted_iota(jnp.int32, (half, half), 0)
    col_ids = lax.broadcasted_iota(jnp.int32, (half, half), 1)
    upper, lower = pl.ds(offset, half), pl.ds(offset + half, half)

    def invert_first():
        work[...] = block[0, upper] + jnp.where(row_ids == col_ids, ridge_ref[0], 0.0)
        first = invert_factor(work)
        inverse[0, :half] = first
        below[...] = dot(block[0, lower], first, NT)

    def invert_second():
        ridge_block = jnp.where(row_ids == col_ids, ridge_ref[0], 0.0)
        work[...] = block[1, lower] + ridge_block - dot(below[...], below[...], NT)
        second = invert_factor(work)
        inverse[1, half:] = second
        inverse[0, half:] = -dot(second, dot(below[...], inverse[0, :half], NN), NN)

    def spread(h):
        for step in range(1, col_count):
            gather(h, step, col_count - step).wait_recv()

        gram_ref[:, pl.ds(h * half, half)] = block[h]

    load.wait()
    multiply(0)
    scatter_start(0)
    multiply(1)
    scatter_start(1)
    spread(0)
    gather_start(1)
    pl.when(is_owner)(invert_first)
    spread(1)

    @pl.when(is_owner)
    def _():
        invert_second()
        for h in range(2):
            for step in range(1, rows_count):
                inverse_copy(h, step).start()

    for h in range(2):
        lanes = pl.ds(h * half, half)

        @pl.when(row_pos == window_owner)
        def _():
            window_ref[:, lanes] = block[h, window_cut]

        @pl.when(row_pos != window_owner)
        def _():
            window_wait(h)
            window_ref[:, lanes] = win[h]

        @pl.when(row_pos != owner)
        def _():
            inverse_copy(h, 1).wait_recv()

    inverse_ref[:, :half] = inverse[0]
    inverse_ref[half:, half:] = inverse[1, half:]
    inverse_ref[:half, half:] = jnp.zeros((half, half), jnp.float32)

    for h in range(2):
        for step in range(1, col_count):
            scatter(h, step).wait_send()
            gather(h, step, 0).wait_send()

        @pl.when(is_owner)
        def _():
            for k in range(steps):
                for copy in owner_copies(h, k):
                    copy.wait_send()
            for step in range(1, rows_count):
                inverse_copy(h, step).wait_send()

        @pl.when(is_far)
        def _():
            for k in range(steps):
                forward(h, k, core).wait_send()

        @pl.when(in_window)
        def _():
            for step in range(1, rows_count):
                window_copy(h, step).wait_send()


def gram_columns(index, rows_count, col_count, tile, ridge, signatures):
    rows, features = signatures.shape
    steps = max(n for n in range(1, 9) if features % (n * 128 * CORES) == 0)
    half = PANEL // 2
    dma = pltpu.SemaphoreType.DMA
    vmem = pl.BlockSpec(memory_space=pltpu.VMEM)
    return pl.pallas_call(
        functools.partial(gram_kernel, index, rows_count, col_count, steps, tile),
        name=f"gram_{index}",
        out_shape=[jax.ShapeDtypeStruct((n, PANEL), jnp.float32) for n in (rows, tile, PANEL)],
        in_specs=[pl.BlockSpec(memory_space=pltpu.SMEM), pl.BlockSpec(memory_space=pl.ANY)],
        out_specs=[vmem] * 3,
        scratch_shapes=[
            pltpu.VMEM((rows, features), jnp.bfloat16),
            pltpu.VMEM((PANEL, features), jnp.bfloat16),
            pltpu.VMEM((2, rows, half), jnp.float32),
            pltpu.VMEM((2, col_count, rows // col_count, half), jnp.float32),
            pltpu.VMEM((2, rows, half), jnp.float32),
            pltpu.VMEM((2, tile, half), jnp.float32),
            pltpu.VMEM((2, PANEL, half), jnp.float32),
            pltpu.VMEM((half, half), jnp.float32),
            pltpu.VMEM((half, half), jnp.float32),
            dma((3,)),
            dma((2, steps, rows_count)), dma((2, steps)),
            dma((2, steps)), dma((2, steps)),
            dma((2, col_count)), dma((2, col_count)),
            dma((2, col_count)), dma((2, col_count)),
            dma((2, rows_count)), dma((2, tile * col_count // rows)),
            dma((2, rows_count)), dma((2,)),
        ],
        compiler_params=pltpu.CompilerParams(
            collective_id=index, has_side_effects=True, vmem_limit_bytes=40 * 1024 * 1024
        ),
    )(ridge, signatures)


def dot(a, b, dims):
    return lax.dot_general(a, b, dims, precision=lax.Precision.HIGHEST, preferred_element_type=jnp.float32)


def invert_factor(work):
    size = work.shape[0]
    segment = size // 4

    def pick(mask, value):
        return jnp.sum(jnp.where(mask, value, 0.0), axis=1, keepdims=True)

    for top in range(0, size, segment):
        active = size - top
        rows = top + lax.broadcasted_iota(jnp.int32, (active, 1), 0)
        lanes = lax.broadcasted_iota(jnp.int32, (active, size), 1)
        lane = lax.broadcasted_iota(jnp.int32, (1, size), 1)

        def pair(i, _):
            k = top + 2 * i
            value = work[top:, :]
            row_0, row_1 = work[pl.ds(k, 1), :], work[pl.ds(k + 1, 1), :]
            at_0, at_1 = lane == k, lane == k + 1
            column_0 = pick(lanes == k, value)
            column_1 = pick(lanes == k + 1, value)
            cross = pick(at_1, row_0)
            over_0 = 1.0 / pick(at_0, row_0)
            ratio = pick(at_0, row_1) * over_0
            over_1 = 1.0 / (pick(at_1, row_1) - ratio * cross)
            unit_0 = jnp.where(at_0, 1.0, row_0)
            next_1 = jnp.where(at_0, 0.0, row_1) - ratio * unit_0
            later = rows > k + 1
            scale_0 = jnp.where(later, column_0 * over_0, 0.0)
            scale_1 = jnp.where(later, (column_1 - scale_0 * cross) * over_1, 0.0)
            base = jnp.where(later & ((lanes == k) | (lanes == k + 1)), 0.0, value)
            work[top:, :] = (
                base - scale_0 * jnp.where(at_1, 0.0, unit_0) - scale_1 * jnp.where(at_1, 1.0, next_1)
            )
            work[pl.ds(k + 1, 1), :] = next_1
            return 0

        lax.fori_loop(0, segment // 2, pair, 0)
    row_ids = lax.broadcasted_iota(jnp.int32, (size, size), 0)
    col_ids = lax.broadcasted_iota(jnp.int32, (size, size), 1)
    value = work[...]
    same = row_ids == col_ids
    unit = jnp.where(row_ids > col_ids, value, jnp.where(same, 1.0, 0.0))
    return unit / jnp.sqrt(pick(same, value))


def update_kernel(
    index_ref, ridge_ref, gram_ref, window_ref, inverse_ref, trailing_ref, factor_ref, updated_ref, full
):
    rows = gram_ref.shape[0]
    share = factor_ref.shape[0]
    start = index_ref[0] * PANEL
    ridge = ridge_ref[0]
    first_row = index_ref[1] * rows
    ids = first_row + lax.broadcasted_iota(jnp.int32, (rows, PANEL), 0)
    panel_ids = start + lax.broadcasted_iota(jnp.int32, (rows, PANEL), 1)
    gram = gram_ref[...] + jnp.where(ids == panel_ids, ridge, 0.0)
    full[...] = jnp.where(ids >= start, dot(gram, inverse_ref[...], NT), 0.0)
    window = dot(window_ref[...], inverse_ref[...], NT)
    updated_ref[...] = trailing_ref[...] - dot(full[...], window, NT)
    factor_ref[...] = full[pl.ds(pl.multiple_of(index_ref[2] * share, share), share), :]


def update(places, ridge, gram, window, inverse, trailing, share):
    vmem = pl.BlockSpec(memory_space=pltpu.VMEM)
    smem = pl.BlockSpec(memory_space=pltpu.SMEM)
    return pl.pallas_call(
        update_kernel,
        name="update",
        out_shape=[
            jax.ShapeDtypeStruct((share, PANEL), jnp.float32),
            jax.ShapeDtypeStruct(trailing.shape, jnp.float32),
        ],
        in_specs=[smem, smem] + [vmem] * 4,
        out_specs=[vmem] * 2,
        scratch_shapes=[pltpu.VMEM(gram.shape, jnp.float32)],
        compiler_params=pltpu.CompilerParams(vmem_limit_bytes=40 * 1024 * 1024),
    )(places, ridge, gram, window, inverse, trailing)


def solution(mesh):
    rows_count, col_count = mesh.shape["row"], mesh.shape["col"]

    def local(signatures, trailing, ridge, panel_index):
        rows, tile = signatures.shape[0], trailing.shape[1]
        panels = (rows * rows_count - tile * col_count) // PANEL
        branches = [
            functools.partial(gram_columns, index, rows_count, col_count, tile) for index in range(1, panels)
        ]
        gram, window, inverse = lax.switch(panel_index[0] - 1, branches, ridge, signatures)
        places = jnp.stack([panel_index[0], lax.axis_index("row"), lax.axis_index("col")]).astype(jnp.int32)
        return tuple(update(places, ridge, gram, window, inverse, trailing, rows // col_count))

    return jax.shard_map(
        local,
        mesh=mesh,
        in_specs=(P("row", "col"), P("row", "col"), P(), P()),
        out_specs=(P(("row", "col"), None), P("row", "col")),
        check_vma=False,
    )
```
